128 devices in a mesh: strip: 8 (over x, z_hi), cuts: 16 (over y, z_lo, core).
Axes of the slice: x: 4, y: 4, z: 4 (z_hi: 2, z_lo: 2; z = z_hi * 2 + z_lo), core: 2. Of those that a mesh axis runs over, the one named last changes fastest.
Arguments:
- start_state: float32 [16, 6, 1024, 512], P('cuts', None, 'strip'), may hold values from -6 to 6
- initial_state: float32 [6, 1024, 512], P(None, 'strip'), may hold values from -6 to 6
- circ_stiff: float32 [1024, 512], P('strip'), may hold values from 0.5 to 2
- axial_stiff: float32 [1024, 512], P('strip'), may hold values from 0.5 to 2
- lumped_mass: float32 [1024, 512], P('strip'), may hold values from 1 to 2
- hoop_stiff: float32 [1024, 512], P('strip'), may hold values from 0.5 to 2
Outputs:
- new_start: float32 [16, 6, 1024, 512], P('cuts', None, 'strip')
- fine_end: float32 [16, 6, 1024, 512], P('cuts', None, 'strip')
The draws below stay inside these ranges and needn't reach their ends.
All inputs are finite; a program needn't handle non-finite values.
Results may differ from the reference program's by a relative error of at most 0.00002.
Values sent between devices are 32-bit elements; how exact they have to be, the bound alone decides.
A program may use at most 192 MiB of HBM per device.

```python
import math
import jax
import jax.numpy as jnp
from jax import lax

NA = 512
NC = 1024
SLICES = 16


def levels(rng, shape, shards, low, largest):
    gain = 1.0
    for axis_at, parts in shards:
        heights = jax.random.uniform(jax.random.fold_in(jax.random.fold_in(rng, 6), axis_at), (parts,), jnp.float32, low / len(shards), largest / len(shards))
        gain = gain * jnp.repeat(jnp.exp(heights), shape[axis_at] // parts).reshape((-1,) + (1,) * (len(shape) - 1 - axis_at))
    return gain


def scatter_about(rng, extent, deviation, reach, cuts=(), kind=jnp.bfloat16):
    values = deviation * jax.random.normal(rng, extent, jnp.float32)
    if cuts:
        values = values * levels(rng, extent, cuts, -0.22, 0.18)
    return jnp.clip(values, -reach, reach).astype(kind)


def setup_inputs(seed: int = 0) -> dict:
    arg_keys = jax.random.split(jax.random.key(seed), 7)
    start_state = scatter_about(arg_keys[0], (SLICES, 6, NC, NA), 1.0, 6.0, ((0, 16), (2, 8)), jnp.float32)
    initial_state = scatter_about(arg_keys[1], (6, NC, NA), 1.0, 6.0, ((1, 8),), jnp.float32)
    circ_stiff = jnp.clip(jnp.exp(math.log(2.0) - 1.3862944 * jax.random.uniform(arg_keys[2], (NC, NA), jnp.float32) ** levels(arg_keys[2], (NC, NA), ((0, 8),), -0.2, 0.2)), 0.5, 2.0)
    axial_stiff = jnp.clip(jnp.exp(math.log(2.0) - 1.3862944 * jax.random.uniform(arg_keys[3], (NC, NA), jnp.float32) ** levels(arg_keys[3], (NC, NA), ((0, 8),), -0.2, 0.2)), 0.5, 2.0)
    lumped_mass = jnp.clip(jnp.exp(math.log(2.0) - 0.6931472 * jax.random.uniform(arg_keys[4], (NC, NA), jnp.float32) ** levels(arg_keys[4], (NC, NA), ((0, 8),), -0.2, 0.2)), 1.0, 2.0)
    hoop_stiff = jnp.clip(jnp.exp(math.log(2.0) - 1.3862944 * jax.random.uniform(arg_keys[5], (NC, NA), jnp.float32) ** levels(arg_keys[5], (NC, NA), ((0, 8),), -0.2, 0.2)), 0.5, 2.0)
    return dict(start_state=start_state, initial_state=initial_state, circ_stiff=circ_stiff, axial_stiff=axial_stiff, lumped_mass=lumped_mass, hoop_stiff=hoop_stiff)


step_length = 0.35
coupling_fine = 0.25


def combine_forces(displace, above_rows, below_rows, circ_stiff, circ_low, axial_stiff, hoop_stiff, coupling):
    zero_col = jnp.zeros_like(displace[:, :, :1])
    forward = jnp.concatenate([displace[:, :, 1:], zero_col], axis=2)
    backward = jnp.concatenate([zero_col, displace[:, :, :-1]], axis=2)
    axial_low = jnp.concatenate([jnp.zeros_like(axial_stiff[:, :1]), axial_stiff[:, :-1]], axis=1)
    summed = circ_stiff * (above_rows - displace) + circ_low * (below_rows - displace)
    summed = summed + axial_stiff * (forward - displace) + axial_low * (backward - displace)
    gradient = 0.5 * (above_rows - below_rows)
    first_comp = summed[0] - coupling * gradient[2]
    third_comp = summed[2] + coupling * gradient[0] - hoop_stiff * displace[2]
    return jnp.stack([first_comp, summed[1], third_comp])


def verlet(current, force_fn, masses, increment, repeats):
    displace = current[:3]
    velocity = current[3:]
    acceleration = force_fn(displace) / masses
    for number in range(repeats):
        half_step = velocity + (0.5 * increment) * acceleration
        displace = displace + increment * half_step
        acceleration = force_fn(displace) / masses
        velocity = half_step + (0.5 * increment) * acceleration
    return jnp.concatenate([displace, velocity], axis=0)


def restrict(field):
    leading = field.shape[:-2]
    rows = field.shape[-2]
    cols = field.shape[-1]
    return field.reshape(leading + (rows // 2, 2, cols // 2, 2)).mean(axis=(-3, -1))


def prolong(field):
    return jnp.repeat(jnp.repeat(field, 2, axis=-2), 2, axis=-1)


def reference(start_state, initial_state, circ_stiff, axial_stiff, lumped_mass, hoop_stiff):
    circ_low = jnp.roll(circ_stiff, 1, axis=0)

    def fine_force(displace):
        return combine_forces(displace, jnp.roll(displace, -1, axis=1), jnp.roll(displace, 1, axis=1),
                              circ_stiff, circ_low, axial_stiff, hoop_stiff, coupling_fine)

    fine_end = lax.map(lambda slice_state: verlet(slice_state, fine_force, lumped_mass, step_length, 2), start_state)
    first_jump = initial_state[None] - start_state[:1]
    mismatch = jnp.concatenate([first_jump, fine_end[:-1] - start_state[1:]], axis=0)
    coarse_circ = restrict(circ_stiff)
    coarse_low = jnp.roll(coarse_circ, 1, axis=0)
    coarse_axial = restrict(axial_stiff)
    coarse_mass = 4.0 * restrict(lumped_mass)
    coarse_hoop = 4.0 * restrict(hoop_stiff)

    def coarse_force(displace):
        return combine_forces(displace, jnp.roll(displace, -1, axis=1), jnp.roll(displace, 1, axis=1),
                              coarse_circ, coarse_low, coarse_axial, coarse_hoop, 2.0 * coupling_fine)

    residue = restrict(mismatch)
    carried = [residue[0]]
    for number in range(1, SLICES):
        carried.append(verlet(carried[-1], coarse_force, coarse_mass, 2.0 * step_length, 1) + residue[number])
    carried = jnp.stack(carried)
    new_start = start_state + mismatch + prolong(carried - residue)
    return new_start, fine_end
```

```python
import jax
import jax.numpy as jnp
from jax import lax
from jax.experimental import pallas as pl
from jax.experimental.pallas import tpu as pltpu
from jax.sharding import PartitionSpec as P

MESH = pl.DeviceIdType.MESH
F32 = jnp.float32
BF16 = jnp.bfloat16
fine_t = 0.35
coarse_t = 0.7
fine_k = 0.25
coarse_k = 0.5

FR, FO = 160, 16
CR, CO = 112, 24


def tile(number):
    return pl.multiple_of(number * 8, 8)


def loop(first, last, body):
    def step(number, carry):
        body(tile(number))
        return carry

    lax.fori_loop(first, last, step, 0)


def along(blocks):
    lane = lax.broadcasted_iota(jnp.int32, (8, 128), 1)
    lefts = [pltpu.roll(block, 127, 1) for block in blocks]
    rights = [pltpu.roll(block, 1, 1) for block in blocks]
    forward = []
    backward = []
    for q in range(len(blocks)):
        ahead = lefts[q] if q == len(blocks) - 1 else jnp.where(lane == 127, lefts[q + 1], lefts[q])
        behind = rights[q] if q == 0 else jnp.where(lane == 0, rights[q - 1], rights[q])
        forward.append(ahead)
        backward.append(behind)
    return forward, backward


def derive(raw, out, r, count, increment, coupling):
    lane = lax.broadcasted_iota(jnp.int32, (8, 128), 1)
    axial = [raw[1, q, pl.ds(r, 8), :] for q in range(count)]
    _, before = along(axial)
    for q in range(count):
        scale = (0.5 * increment * increment) / raw[2, q, pl.ds(r, 8), :]
        circ = raw[0, q, pl.ds(r, 8), :] * scale
        below = raw[0, q, pl.ds(r - 1, 8), :] * scale
        ax = axial[q] * scale
        low = before[q] * scale
        if q == 0:
            low = jnp.where(lane == 0, 0.0, low)
        diagonal = circ + below + ax + low
        out[0, q, pl.ds(r, 8), :] = circ
        out[1, q, pl.ds(r, 8), :] = below
        out[2, q, pl.ds(r, 8), :] = jnp.where(lane == 127, 0.0, ax) if q == count - 1 else ax
        out[3, q, pl.ds(r, 8), :] = low
        out[4, q, pl.ds(r, 8), :] = diagonal
        out[5, q, pl.ds(r, 8), :] = diagonal + raw[3, q, pl.ds(r, 8), :] * scale
        out[6, q, pl.ds(r, 8), :] = scale * (0.5 * coupling)


def pull(load, coefs, r, count, kinds):
    result = []
    edges = []
    for i, kind in enumerate(kinds):
        blocks = [load(i, q, 0) for q in range(count)]
        forward, backward = along(blocks)
        values = []
        sides = []
        for q in range(count):
            above = load(i, q, 1)
            below = load(i, q, -1)
            value = coefs[0, q, pl.ds(r, 8), :] * above + coefs[1, q, pl.ds(r, 8), :] * below
            value = value + coefs[2, q, pl.ds(r, 8), :] * forward[q]
            value = value + coefs[3, q, pl.ds(r, 8), :] * backward[q]
            value = value - coefs[5 if kind == 2 else 4, q, pl.ds(r, 8), :] * blocks[q]
            values.append(value)
            sides.append(above - below)
        result.append(values)
        edges.append(sides)
    if 2 in kinds:
        i0, i2 = kinds.index(0), kinds.index(2)
        for q in range(count):
            couple = coefs[6, q, pl.ds(r, 8), :]
            result[i0][q] = result[i0][q] - couple * edges[i2][q]
            result[i2][q] = result[i2][q] + couple * edges[i0][q]
    return result


def split_dot(x, picks):
    first = x.astype(BF16)
    rest = x - first.astype(F32)
    second = rest.astype(BF16)
    third = (rest - second.astype(F32)).astype(BF16)
    total = jnp.dot(third, picks, preferred_element_type=F32) + jnp.dot(second, picks, preferred_element_type=F32)
    return total + jnp.dot(first, picks, preferred_element_type=F32)


def pair_picks(value, down):
    shape = (256, 128) if down else (128, 256)
    long = lax.broadcasted_iota(jnp.int32, shape, 0 if down else 1)
    short = lax.broadcasted_iota(jnp.int32, shape, 1 if down else 0)
    hit = (long == 2 * short) | (long == 2 * short + 1)
    return jnp.where(hit, value, 0.0).astype(BF16)


def restricted(ref, plane, half, rows, picks):
    parts = [ref[plane, 2 * half + q, pl.ds(0, rows, 2), :] + ref[plane, 2 * half + q, pl.ds(1, rows, 2), :] for q in range(2)]
    return split_dot(jnp.concatenate(parts, axis=1), picks)


def barrier_with(devices):
    barrier = pltpu.get_barrier_semaphore()
    for device in devices:
        pl.semaphore_signal(barrier, inc=1, device_id=device, device_id_type=MESH)
    return lambda: pl.semaphore_wait(barrier, len(devices))


def fine_kernel(
    start, initial, circ, axial, mass, hoop, end, step_out, coarse_out,
    data, other, first, coefs, small, small_next, small_coefs, load_sem, send_sem, recv_sem,
):
    me = lax.axis_index("strip")
    strips = lax.axis_size("strip")
    position = lax.axis_index("cuts")
    above = {"strip": lax.rem(me + 1, strips)}
    below = {"strip": lax.rem(me + strips - 1, strips)}
    arrived = barrier_with([below, above])
    loads = []
    for q in range(4):
        lanes = slice(128 * q, 128 * q + 128)
        loads.append(pltpu.make_async_copy(start.at[0, :, :, lanes], data.at[0:6, q, FO:FO + 128], load_sem.at[len(loads)]))
        for n, field in enumerate((circ, axial, mass, hoop)):
            loads.append(pltpu.make_async_copy(field.at[:, lanes], data.at[6 + n, q, FO:FO + 128], load_sem.at[len(loads)]))
    extra = [
        pltpu.make_async_copy(initial.at[:, :, 128 * q:128 * q + 128], first.at[:, q, FO:FO + 128], load_sem.at[len(loads) + q])
        for q in range(4)
    ]
    for copy in loads:
        copy.start()

    @pl.when(position == 0)
    def _():
        for copy in extra:
            copy.start()

    def edges(ref, at):
        return [
            pltpu.make_async_remote_copy(
                ref.at[:, :, FO:FO + 8], ref.at[:, :, FO + 128:FO + 136], send_sem.at[at], recv_sem.at[at],
                device_id=below, device_id_type=MESH,
            ),
            pltpu.make_async_remote_copy(
                ref.at[:, :, FO + 120:FO + 128], ref.at[:, :, FO - 8:FO], send_sem.at[at + 1], recv_sem.at[at + 1],
                device_id=above, device_id_type=MESH,
            ),
        ]

    for copy in loads:
        copy.wait()
    arrived()
    swaps = edges(data, 0)
    for copy in swaps:
        copy.start()
    swaps_first = edges(first, 2)

    @pl.when(position == 0)
    def _():
        for copy in extra:
            copy.wait()
        for copy in swaps_first:
            copy.start()

    for copy in swaps:
        copy.wait()
    raw = data.at[6:10]
    loop(1, 19, lambda r: derive(raw, coefs, r, 4, fine_t, fine_k))
    picks = pair_picks(0.25, True)

    def shrink_start(plane, carry):
        for half in range(2):
            small[plane, half, pl.ds(16, 80), :] = restricted(data, plane, half, 80, picks)
        return carry

    lax.fori_loop(0, 10, shrink_start, 0)

    @pl.when(position == 0)
    def _():
        for copy in swaps_first:
            copy.wait()

        def shrink_first(plane, carry):
            for half in range(2):
                small[plane, half, pl.ds(16, 80), :] = small[plane, half, pl.ds(16, 80), :] - restricted(first, plane, half, 80, picks)
            return carry

        lax.fori_loop(0, 6, shrink_first, 0)

    def fine_step(r, source, target, gain, incoming):
        pulls = pull(lambda i, q, by: source[i, q, pl.ds(r + by, 8), :], coefs, r, 4, (0, 1, 2))
        for i in range(3):
            for q in range(4):
                held = data[3 + i, q, pl.ds(r, 8), :]
                if incoming:
                    held = held * fine_t
                moved = held + pulls[i][q] * gain if gain != 1 else held + pulls[i][q]
                if target is None:
                    data[3 + i, q, pl.ds(r, 8), :] = moved * (1.0 / fine_t)
                else:
                    data[3 + i, q, pl.ds(r, 8), :] = moved
                    target[i, q, pl.ds(r, 8), :] = source[i, q, pl.ds(r, 8), :] + moved

    shift = data.at[0:3]
    loop(1, 19, lambda r: fine_step(r, shift, other, 1, True))
    loop(1, 19, lambda r: fine_step(r, other, shift, 2, False))
    loop(1, 19, lambda r: fine_step(r, shift, None, 1, False))
    stores = [
        pltpu.make_async_copy(data.at[0:6, q, FO:FO + 128], end.at[0, :, :, 128 * q:128 * q + 128], load_sem.at[q])
        for q in range(4)
    ]
    for copy in stores:
        copy.start()

    small_raw = small.at[6:10]

    def shrink_end(plane, carry):
        for half in range(2):
            small_next[plane, half, pl.ds(16, 80), :] = restricted(data, plane, half, 80, picks)
        return carry

    lax.fori_loop(0, 6, shrink_end, 0)

    def coarse_setup(r):
        for q in range(2):
            for n in (2, 3):
                small_raw[n, q, pl.ds(r, 8), :] = 4.0 * small_raw[n, q, pl.ds(r, 8), :]
            for n in range(4):
                coarse_out[n, q, pl.ds(r, 8), :] = small_raw[n, q, pl.ds(r, 8), :]

    loop(2, 12, coarse_setup)
    loop(2, 12, lambda r: derive(small_raw, small_coefs, r, 2, coarse_t, coarse_k))

    def coarse_first(r):
        pulls = pull(lambda i, q, by: small[i, q, pl.ds(r + by, 8), :], small_coefs, r, 2, (0, 1, 2))
        for i in range(3):
            for q in range(2):
                moved = coarse_t * small[3 + i, q, pl.ds(r, 8), :] + pulls[i][q]
                small[3 + i, q, pl.ds(r, 8), :] = moved
                first[i, q, pl.ds(r, 8), :] = small[i, q, pl.ds(r, 8), :] + moved

    def coarse_last(r):
        pulls = pull(lambda i, q, by: first[i, q, pl.ds(r + by, 8), :], small_coefs, r, 2, (0, 1, 2))
        for i in range(3):
            for q in range(2):
                at_w, at_p = ((0, 2), (4, 5), (1, 3))[i]
                moved = small[3 + i, q, pl.ds(r, 8), :] + pulls[i][q]
                step_out[at_w, q, pl.ds(r, 8), :] = small_next[i, q, pl.ds(r, 8), :] - first[i, q, pl.ds(r, 8), :]
                step_out[at_p, q, pl.ds(r, 8), :] = coarse_t * small_next[3 + i, q, pl.ds(r, 8), :] - moved

    loop(2, 12, coarse_first)
    loop(2, 12, coarse_last)
    for copy in stores:
        copy.wait()


def scan_body(system, step_in, coarse_in, out, raw, coefs, got, p_low, p_high, total, came, begin, even, odd, spare_a, spare_b, swapped, send_sem, recv_sem):
    me = lax.axis_index("strip")
    strips = lax.axis_size("strip")
    position = lax.axis_index("cuts")
    y = position // 4
    z = lax.rem(position // 2, 2)
    above = lax.rem(me + 1, strips)
    below = lax.rem(me + strips - 1, strips)
    sibling = {"cuts": position + 1 - 2 * system}
    across = position + 2 - 4 * z
    up = lax.rem(position + 4, 16)
    down = lax.rem(position + 12, 16)
    kinds = ((0, 2), (1,))[system]
    comps = len(kinds)
    planes = 2 * comps
    own = slice(CO, CO + 64)

    def send(source, target, at, device):
        return pltpu.make_async_remote_copy(
            source, target, send_sem.at[at], recv_sem.at[at], device_id=device, device_id_type=MESH
        )

    def body_copy(source, target, at, cut):
        return send(source.at[0:planes, :, own], target.at[0:planes, :, own], at, {"cuts": cut})

    def to_below(source, target, at, cut, rows):
        return send(
            source.at[0:planes, :, CO:CO + rows], target.at[0:planes, :, CO + 64:CO + 64 + rows], at,
            {"strip": below, "cuts": cut},
        )

    def to_above(source, target, at, cut, rows):
        return send(
            source.at[0:planes, :, CO + 64 - rows:CO + 64], target.at[0:planes, :, CO - rows:CO], at,
            {"strip": above, "cuts": cut},
        )

    def three(source, target, at, cut, rows):
        return [to_below(source, target, at + 1, cut, rows), to_above(source, target, at + 2, cut, rows), body_copy(source, target, at, cut)]

    def start(copies):
        for copy in copies:
            copy.start()

    def sent(copies):
        for copy in copies:
            copy.wait_send()

    def landed(copies):
        for copy in copies:
            copy.wait_recv()

    def load(ref, base=0):
        return lambda r: (lambda i, q, by: ref[base + i, q, pl.ds(r + by, 8), :])

    def advance(source, target, gain, first, last, base=0):
        def body(r):
            pulls = pull(load(source, base)(r), coefs, r, 2, kinds)
            for i in range(comps):
                for q in range(2):
                    moved = source[base + comps + i, q, pl.ds(r, 8), :] + (pulls[i][q] * gain if gain != 1 else pulls[i][q])
                    target[comps + i, q, pl.ds(r, 8), :] = moved
                    target[i, q, pl.ds(r, 8), :] = source[base + i, q, pl.ds(r, 8), :] + moved

        loop(first, last, body)

    def settle(source, addend, target, first, last, base=0):
        def body(r):
            pulls = pull(load(source)(r), coefs, r, 2, kinds)
            for i in range(comps):
                for q in range(2):
                    target[comps + i, q, pl.ds(r, 8), :] = (
                        source[comps + i, q, pl.ds(r, 8), :] + pulls[i][q] + addend[base + comps + i, q, pl.ds(r, 8), :]
                    )
                    target[i, q, pl.ds(r, 8), :] = source[i, q, pl.ds(r, 8), :] + addend[base + i, q, pl.ds(r, 8), :]

        loop(first, last, body)

    def propagate(source, steps, addend, target, first, last, base=0, add_base=0, kept=None):
        spares = (spare_a, spare_b)
        for n in range(steps):
            advance(source if n == 0 else spares[(n + 1) % 2], spares[n % 2], 1 if n == 0 else 2, first, last, base if n == 0 else 0)
        settle(spares[(steps + 1) % 2], addend, target, *(kept or (first, last)), add_base)

    mine = 4 * system
    pair = send(step_in.at[4:6], got.at[0:2], 0, sibling) if system == 0 else send(step_in.at[0:4], got.at[0:4], 0, sibling)
    pair_in = send(step_in.at[0:4], got.at[0:4], 0, sibling) if system == 0 else send(step_in.at[4:6], got.at[0:2], 0, sibling)
    start([pair])
    stiff = [
        send(coarse_in.at[:, :, CO:CO + 16], raw.at[:, :, CO + 64:CO + 80], 1, {"strip": below}),
        send(coarse_in.at[:, :, CO + 48:CO + 64], raw.at[:, :, CO - 16:CO], 2, {"strip": above}),
    ]
    start(stiff)

    def copy_in(r):
        for n in range(4):
            for q in range(2):
                raw[n, q, pl.ds(r, 8), :] = coarse_in[n, q, pl.ds(r, 8), :]

    loop(3, 11, copy_in)
    landed(stiff)
    loop(1, 13, lambda r: derive(raw, coefs, r, 2, coarse_t, coarse_k))
    landed([pair_in])
    if system == 0:
        early, early_at, late, late_at = step_in, 0, got, 0
    else:
        early, early_at, late, late_at = got, 0, step_in, 4

    low_near = [to_below(p_low, p_low, 4, position, 8), to_above(p_low, p_low, 5, position, 8)]
    low_far = [to_below(p_low, p_low, 6, across, 8), to_above(p_low, p_low, 7, across, 8), body_copy(p_low, p_low, 3, across)]
    high_far = [body_copy(p_high, p_high, 3, across)]

    @pl.when(z == 0)
    def _():
        propagate(early, 1, late, p_low, 2, 12, early_at, late_at, (3, 11))
        start(low_near + low_far)
        landed(high_far + low_near)

    @pl.when(z == 1)
    def _():
        propagate(early, 1, late, p_high, 2, 12, early_at, late_at, (3, 11))
        start(high_far)
        landed(low_far)

    propagate(p_low, 2, p_high, total, 2, 12)
    next_up = three(total, came, 8, up, 8)
    next_down = three(total, came, 11, down, 16)
    final_up = three(even, begin, 14, up, 8)

    @pl.when(y == 0)
    def _():
        start(next_up + next_down)

        def clear(r):
            for n in range(planes):
                for q in range(2):
                    begin[n, q, pl.ds(r, 8), :] = jnp.zeros((8, 128), F32)

        loop(2, 12, clear)

    @pl.when(y == 1)
    def _():
        start(next_up)
        landed(next_up)
        propagate(came, 4, total, even, 2, 12)
        start(final_up)

        def keep(r):
            for n in range(planes):
                for q in range(2):
                    begin[n, q, pl.ds(r, 8), :] = came[n, q, pl.ds(r, 8), :]

        loop(2, 12, keep)

    @pl.when(y == 2)
    def _():
        landed(next_up)
        propagate(came, 4, total, even, 2, 12)
        start(final_up)
        landed(final_up)

    @pl.when(y == 3)
    def _():
        landed(next_down)
        for n in range(8):
            advance((came, spare_a, spare_b)[0 if n == 0 else 1 + (n + 1) % 2], (spare_a, spare_b)[n % 2], 1 if n == 0 else 2, 1, 13)
        landed(final_up)
        settle(spare_b, begin, odd, 2, 12)

        def keep(r):
            for n in range(planes):
                for q in range(2):
                    begin[n, q, pl.ds(r, 8), :] = odd[n, q, pl.ds(r, 8), :]

        loop(2, 12, keep)

    @pl.when((y == 1) | (y == 2))
    def _():
        sent(final_up)

    @pl.when(z == 0)
    def _():
        def keep(r):
            for n in range(planes):
                for q in range(2):
                    even[n, q, pl.ds(r, 8), :] = begin[n, q, pl.ds(r, 8), :]

        loop(2, 12, keep)

    @pl.when(z == 1)
    def _():
        propagate(begin, 2, p_low, even, 2, 12)

    propagate(even, 1, early, odd, 2, 12, 0, early_at)
    swap = send((odd if system == 0 else even).at[0:planes, :, own], swapped.at[0:planes], 17, sibling)
    swap_in = send(came.at[0:6 - planes, :, own], swapped.at[0:6 - planes], 17, sibling)

    start([swap])
    kept = even if system == 0 else odd
    for n in range(planes):
        out[mine + n] = kept[n, :, CO:CO + 64, :]
    landed([swap_in])
    for n in range(6 - planes):
        out[(4 if system == 0 else 0) + n] = swapped[n]

    sent([pair] + stiff + [swap])

    @pl.when(z == 0)
    def _():
        sent(low_near + low_far)

    @pl.when(z == 1)
    def _():
        sent(high_far)

    @pl.when(y == 0)
    def _():
        sent(next_up + next_down)

    @pl.when(y == 1)
    def _():
        sent(next_up)


def scan_kernel(step_in, coarse_in, out, *scratch):
    me = lax.axis_index("strip")
    strips = lax.axis_size("strip")
    position = lax.axis_index("cuts")
    core = lax.rem(position, 2)
    z = lax.rem(position // 2, 2)
    above = lax.rem(me + 1, strips)
    below = lax.rem(me + strips - 1, strips)
    across = position + 2 - 4 * z
    up = lax.rem(position + 4, 16)
    down = lax.rem(position + 12, 16)
    devices = [{"cuts": position + 1 - 2 * core}, {"strip": above}, {"strip": below}]
    for cut in (across, up, down):
        devices += [{"cuts": cut}, {"strip": above, "cuts": cut}, {"strip": below, "cuts": cut}]
    barrier_with(devices)()
    for system in range(2):
        @pl.when(core == system)
        def _(system=system):
            scan_body(system, step_in, coarse_in, out, *scratch)


def compose_kernel(came, coarse, initial, out, data, load_sem):
    position = lax.axis_index("cuts")

    def copies(source, back):
        pairs = [(source.at[:, :, 128 * q:128 * q + 128], data.at[:, q]) for q in range(4)]
        return [pltpu.make_async_copy(b, a, load_sem.at[q]) if back else pltpu.make_async_copy(a, b, load_sem.at[q]) for q, (a, b) in enumerate(pairs)]

    @pl.when(position == 0)
    def _():
        for copy in copies(initial, False):
            copy.start()
        for copy in copies(initial, False):
            copy.wait()

    @pl.when(position > 0)
    def _():
        for copy in copies(came, False):
            copy.start()
        for copy in copies(came, False):
            copy.wait()
        shrink = pair_picks(0.25, True)
        grow = pair_picks(1.0, False)
        for plane in range(6):
            at, gain = ((0, 1.0), (4, 1.0), (1, 1.0), (2, 1.0 / coarse_t), (5, 1.0 / coarse_t), (3, 1.0 / coarse_t))[plane]
            for half in range(2):
                wanted = coarse[at, half] * gain if plane >= 3 else coarse[at, half]
                spread = split_dot(wanted - restricted(data, plane, half, 64, shrink), grow)
                for q in range(2):
                    for odd in range(2):
                        rows = pl.ds(odd, 64, 2)
                        data[plane, 2 * half + q, rows, :] = data[plane, 2 * half + q, rows, :] + spread[:, 128 * q:128 * q + 128]

    for copy in copies(out.at[0], True):
        copy.start()
    for copy in copies(out.at[0], True):
        copy.wait()


def per_device(start_state, initial_state, circ_stiff, axial_stiff, lumped_mass, hoop_stiff):
    anywhere = pl.BlockSpec(memory_space=pl.ANY)
    inside = pl.BlockSpec(memory_space=pltpu.VMEM)
    field = lambda n, q, rows: pltpu.VMEM((n, q, rows, 128), F32)
    fine_end, step, stiff = pl.pallas_call(
        fine_kernel,
        name="fine",
        out_shape=(
            jax.ShapeDtypeStruct((1, 6, 128, 512), F32),
            jax.ShapeDtypeStruct((6, 2, CR, 128), F32),
            jax.ShapeDtypeStruct((4, 2, CR, 128), F32),
        ),
        in_specs=[anywhere] * 6,
        out_specs=(anywhere, inside, inside),
        scratch_shapes=[
            field(10, 4, FR), field(3, 4, FR), field(6, 4, FR), field(7, 4, FR),
            field(10, 2, CR), field(6, 2, CR), field(7, 2, CR),
            pltpu.SemaphoreType.DMA((24,)), pltpu.SemaphoreType.DMA((4,)), pltpu.SemaphoreType.DMA((4,)),
        ],
        compiler_params=pltpu.CompilerParams(collective_id=0, has_side_effects=True),
        cost_estimate=pl.CostEstimate(flops=30_000_000, bytes_accessed=8_000_000, transcendentals=0),
    )(start_state, initial_state, circ_stiff, axial_stiff, lumped_mass, hoop_stiff)
    cuts = lax.axis_size("cuts")
    came = lax.ppermute(fine_end[0], "cuts", [(i, i + 1) for i in range(cuts - 1)])
    coarse = pl.pallas_call(
        scan_kernel,
        name="scan",
        out_shape=jax.ShapeDtypeStruct((6, 2, 64, 128), F32),
        in_specs=[inside] * 2,
        out_specs=inside,
        scratch_shapes=[field(4, 2, CR), field(7, 2, CR)] + [field(4, 2, CR)] * 10 + [
            field(4, 2, 64),
            pltpu.SemaphoreType.DMA((18,)), pltpu.SemaphoreType.DMA((18,)),
        ],
        compiler_params=pltpu.CompilerParams(collective_id=1, has_side_effects=True),
        cost_estimate=pl.CostEstimate(flops=60_000_000, bytes_accessed=100_000_000, transcendentals=0),
    )(step, stiff)
    new_start = pl.pallas_call(
        compose_kernel,
        name="compose",
        out_shape=jax.ShapeDtypeStruct((1, 6, 128, 512), F32),
        in_specs=[anywhere, inside, anywhere],
        out_specs=anywhere,
        scratch_shapes=[field(6, 4, 128), pltpu.SemaphoreType.DMA((4,))],
        cost_estimate=pl.CostEstimate(flops=1_000_000, bytes_accessed=4_000_000, transcendentals=0),
    )(came, coarse, initial_state)
    return (new_start, fine_end)


def solution(mesh):
    placed = (
        P("cuts", None, "strip", None),
        P(None, "strip", None),
        P("strip", None),
        P("strip", None),
        P("strip", None),
        P("strip", None),
    )
    return jax.shard_map(
        per_device,
        mesh=mesh,
        in_specs=placed,
        out_specs=(P("cuts", None, "strip", None), P("cuts", None, "strip", None)),
        check_vma=False,
    )
```
